32 devices in a mesh: dp: 8 (over y, x, core), seq: 4 (over z).
Axes of the slice: x: 2, y: 2, z: 4, core: 2. Of those that a mesh axis runs over, the one named last changes fastest.
Arguments:
- tokens: int32 [8, 1024], P('dp', 'seq'), may hold values from 0 to 3
- embedding: float32 [4, 384], replicated, may hold values from -6 to 6
- gain_in: float32 [384], replicated, may hold values from 0.5 to 1.5
- conv_taps: float32 [384, 4], replicated, may hold values from -3 to 3
- long_filter: float32 [384, 1024], P('seq'), may hold values from -6 to 6
- gain_mid: float32 [384], replicated, may hold values from 0.5 to 1.5
- mlp_weights: bfloat16 [2304, 384], replicated, may hold values from -0.3125 to 0.3125
- cotangent: bfloat16 [8, 768, 1024], P('dp', None, 'seq'), may hold values from -6 to 6
Outputs:
- layer_out: bfloat16 [8, 768, 1024], P('dp', None, 'seq')
- grad_embedding: float32 [4, 384], replicated
- grad_gain_in: float32 [384], replicated
- grad_conv: float32 [384, 4], replicated
- grad_filter: float32 [384, 1024], P('seq')
- grad_gain_mid: float32 [384], replicated
- grad_mlp: float32 [2304, 384], P('dp', 'seq')
The draws below stay inside these ranges and needn't reach their ends.
All inputs are finite; a program needn't handle non-finite values.
Results may differ from the reference program's by a relative error of at most 0.03.
Values may be sent and summed in bfloat16 or wider, within the bound.
A program may use at most 64 MiB of HBM per device.

```python
from functools import partial
import jax
import jax.numpy as jnp
from jax import lax

D = 384
FF = 768
GROUP = 1024
KW = 4
LEN = 1024
BATCH = 8


def plant(values, key, least, top_value):
    extent = values.shape
    spot = [jax.random.randint(jax.random.fold_in(key, axis), (), 0, extent[axis]) for axis in range(len(extent))]
    values = values.at[tuple(spot)].set(least)
    longest = extent.index(max(extent))
    spot[longest] = (spot[longest] + 1) % extent[longest]
    return values.at[tuple(spot)].set(top_value)


def steps_of(own_key, shape, shards, least, high):
    loudness, own = 1.0, jax.random.fold_in(own_key, 6)
    for axis_at, shards_of in shards:
        draws = jnp.exp(jax.random.uniform(jax.random.fold_in(own, axis_at), (shards_of,), jnp.float32, least / len(shards), high / len(shards)))
        loudness = loudness * jnp.repeat(draws, shape[axis_at] // shards_of).reshape([-1 if axis == axis_at else 1 for axis in range(len(shape))])
    return loudness


def bell_draw(stream_key, shape, spread, reach, cuts=(), kind=jnp.bfloat16):
    values = spread * jax.random.normal(stream_key, shape, jnp.float32)
    if cuts:
        values = values * steps_of(stream_key, shape, cuts, -0.22, 0.18)
    return jnp.clip(values, -reach, reach).astype(kind)


def setup_inputs(seed: int = 0) -> dict:
    streams_of = jax.random.split(jax.random.key(seed), 9)
    tokens = plant(jax.random.randint(streams_of[0], (BATCH, LEN), 0, 4), jax.random.fold_in(streams_of[0], 1), 0, 3).astype(jnp.int32)
    embedding = bell_draw(streams_of[1], (4, D), 1.0, 6.0, (), jnp.float32)
    gain_in = jnp.clip(1.0 + 0.1 * jax.random.normal(streams_of[2], (D,), jnp.float32), 0.5, 1.5)
    conv_taps = bell_draw(streams_of[3], (D, KW), KW ** -0.5, 3.0, (), jnp.float32)
    long_filter = bell_draw(streams_of[4], (D, GROUP), 1.0, 6.0, ((0, 4),), jnp.float32)
    gain_mid = jnp.clip(1.0 + 0.1 * jax.random.normal(streams_of[5], (D,), jnp.float32), 0.5, 1.5)
    mlp_weights = bell_draw(streams_of[6], (3 * FF, D), D ** -0.5, 0.3125)
    cotangent = bell_draw(streams_of[7], (BATCH, 2 * D, LEN), 1.0, 6.0, ((0, 8), (2, 4)))
    return dict(tokens=tokens, embedding=embedding, gain_in=gain_in, conv_taps=conv_taps, long_filter=long_filter, gain_mid=gain_mid, mlp_weights=mlp_weights, cotangent=cotangent)


def dct_table(length):
    freq = jnp.arange(length, dtype=jnp.int32)[:, None]
    place = jnp.arange(length, dtype=jnp.int32)[None, :]
    phase = (2 * place + 1) * freq % (4 * length)
    weight = jnp.where(freq == 0, jnp.sqrt(1.0 / length), jnp.sqrt(2.0 / length))
    angle = jnp.pi * phase.astype(jnp.float32) / (2 * length)
    return (weight * jnp.cos(angle)).astype(jnp.bfloat16)

def rms_gain(values, gain):
    scale = lax.rsqrt(lax.optimization_barrier(jnp.mean(values * values, axis=-2, keepdims=True)) + 1e-06)
    return (values * scale * gain[:, None]).astype(jnp.bfloat16)

def lookup_norm(embedding, gain_in, onehot):
    residual = jnp.einsum('kd,sbkl->sbdl', embedding, onehot, precision=lax.Precision.HIGHEST)
    return (residual, rms_gain(residual, gain_in))

def conv_before(padded, conv_taps):
    rim_width = conv_taps.shape[1] - 1
    length = padded.shape[-1] - rim_width
    summed = conv_taps[:, 0][:, None] * padded[..., rim_width:rim_width + length]
    for tap_index in range(1, rim_width + 1):
        start = rim_width - tap_index
        summed = summed + conv_taps[:, tap_index][:, None] * padded[..., start:start + length]
    return summed.astype(jnp.bfloat16)

def group_filter(mixed, long_filter, dct_rows):
    strands, batch, channels, length = mixed.shape
    block_len = dct_rows.shape[0]
    blocks = mixed.astype(jnp.float32).reshape(strands, batch, channels, length // block_len, block_len)
    table_f = dct_rows.astype(jnp.float32)
    spectrum = jnp.einsum('sbdni,ki->sbdnk', blocks, table_f, precision=lax.Precision.HIGHEST).astype(jnp.bfloat16)
    scaled = (long_filter[None, None, :, None, :] * spectrum.astype(jnp.float32)).astype(jnp.bfloat16)
    restored = jnp.einsum('sbdnk,ki->sbdni', scaled.astype(jnp.float32), table_f, precision=lax.Precision.HIGHEST)
    return restored.astype(jnp.bfloat16).reshape(strands, batch, channels, length)

def mid_norm(residual, filtered, gain_mid):
    level = residual + filtered.astype(jnp.float32)
    return (level, rms_gain(level, gain_mid))

def feed_forward(level, normed_mid, weights):
    projected = jnp.einsum('fd,sbdl->sbfl', weights[:2 * FF], normed_mid.astype(jnp.float32), precision=lax.Precision.HIGHEST).astype(jnp.bfloat16)
    both_parts = projected.astype(jnp.float32)
    gate_in = both_parts[:, :, :FF]
    up_value = both_parts[:, :, FF:]
    activated = (jax.nn.silu(gate_in) * up_value).astype(jnp.bfloat16)
    down = jnp.einsum('fd,sbfl->sbdl', weights[2 * FF:], activated.astype(jnp.float32), precision=lax.Precision.HIGHEST)
    return (level + down).astype(jnp.bfloat16)

def strand_layer(base_ids, dct_rows, embedding, gain_in, conv_taps, long_filter, gain_mid, weights):
    strands = jnp.stack([base_ids, 3 - jnp.flip(base_ids, 0)])[:, None, :]
    onehot = (strands[:, :, None, :] == jnp.arange(4, dtype=jnp.int32)[None, None, :, None]).astype(jnp.float32)
    residual, normed = lookup_norm(embedding, gain_in, onehot)
    padded = jnp.pad(normed.astype(jnp.float32), ((0, 0), (0, 0), (0, 0), (KW - 1, 0)))
    mixed = conv_before(padded, conv_taps)
    filtered = group_filter(mixed, long_filter, dct_rows)
    level, normed_mid = mid_norm(residual, filtered, gain_mid)
    result = feed_forward(level, normed_mid, weights)
    return jnp.concatenate([result[0, 0], jnp.flip(result[1, 0], (0, 1))], 0)

def reference(tokens, embedding, gain_in, conv_taps, long_filter, gain_mid, mlp_weights, cotangent):
    dct_rows = dct_table(GROUP)
    params = (embedding, gain_in, conv_taps, long_filter, gain_mid, mlp_weights.astype(jnp.float32))

    def one_sequence(running, sliced):
        base_ids, seq_cot = sliced
        layer_part, pullback = jax.vjp(partial(strand_layer, base_ids, dct_rows), *params)
        gradients = pullback(seq_cot)
        return (tuple((summed_grad + fresh_grad for summed_grad, fresh_grad in zip(running, gradients))), layer_part)
    zeros = tuple((jnp.zeros(param.shape, jnp.float32) for param in params))
    totals, layer_out = lax.scan(one_sequence, zeros, (tokens, cotangent))
    return (layer_out, totals[0], totals[1], totals[2], totals[3], totals[4], totals[5])
```

```python
import jax
import jax.numpy as jnp
import numpy as np
from jax import lax
from jax.sharding import PartitionSpec as P

F32 = jnp.float32
BF16 = jnp.bfloat16


def dct_table(length):
    freq = np.arange(length)[:, None]
    place = np.arange(length)[None, :]
    phase = (2 * place + 1) * freq % (4 * length)
    weight = np.where(freq == 0, np.sqrt(1.0 / length), np.sqrt(2.0 / length))
    return (weight * np.cos(np.pi * phase / (2 * length))).astype(np.float32).astype(BF16)


def dot(a, b, dims):
    return lax.dot_general(a, b, (dims, ((), ())), preferred_element_type=F32)


def compute(ids_block, ids_own, q_rows, q_own, embedding, gain_in, conv_taps, filt, gain_mid, mlp, cot):
    taps = conv_taps.shape[1]
    channels = embedding.shape[1]
    block_len = q_rows.shape[0]
    hidden = mlp.shape[0] // 3
    local_len = ids_own.shape[0]
    base_scale = lax.rsqrt(jnp.mean(embedding * embedding, axis=1, keepdims=True) + 1e-6)
    base_norm = (embedding * base_scale * gain_in[None, :]).astype(BF16)
    kmer = (conv_taps[:, :, None] * base_norm.astype(F32).T[:, None, :]).reshape(channels, -1).astype(BF16)
    bases = jnp.arange(4, dtype=jnp.int32)[:, None]
    rim = taps - 1
    fwd = [ids_block[rim - k : rim - k + block_len] for k in range(taps)]
    rev = [3 - ids_block[rim + k : rim + k + block_len] for k in range(taps)]
    hot = jnp.concatenate([(row[None, :] == bases) for row in fwd + rev], 0).astype(BF16)
    hot_spec = dot(hot, q_rows, ((1,), (1,))).astype(BF16)
    half = 4 * taps
    specs = [dot(kmer, hot_spec[s * half : (s + 1) * half], ((1,), (0,))).astype(BF16) for s in range(2)]
    scaled = [(filt * spec.astype(F32)).astype(BF16) for spec in specs]
    filtered = jnp.concatenate([dot(one, q_own, ((1,), (0,))) for one in scaled], 1)
    both = jnp.concatenate([ids_own, 3 - ids_own])
    emb_cols = embedding.T
    residual = jnp.zeros((channels, 2 * local_len), F32)
    for a in range(4):
        residual = residual + jnp.where(both[None, :] == a, emb_cols[:, a : a + 1], 0.0)
    level = residual + filtered
    mid_scale = lax.rsqrt(jnp.mean(level * level, axis=0, keepdims=True) + 1e-6)
    unit = level * mid_scale
    normed = (unit * gain_mid[:, None]).astype(BF16)
    w_in, w_down = mlp[: 2 * hidden], mlp[2 * hidden :]
    proj = dot(w_in, normed, ((1,), (0,))).astype(BF16).astype(F32)
    gate, up = proj[:hidden], proj[hidden:]
    sig = jax.nn.sigmoid(gate)
    act = (gate * sig * up).astype(BF16)
    combined = (level + dot(w_down, act, ((0,), (0,)))).astype(BF16)
    layer_out = jnp.concatenate([combined[:, :local_len], jnp.flip(combined[:, local_len:], 0)], 0)
    back = jnp.concatenate([cot[:channels], jnp.flip(cot[channels:], 0)], 1)
    d_act = dot(w_down, back, ((1,), (0,)))
    d_gate = d_act * up * sig * (1.0 + gate * (1.0 - sig))
    d_up = d_act * gate * sig
    d_proj = jnp.concatenate([d_gate, d_up], 0).astype(BF16)
    d_normed = dot(w_in, d_proj, ((0,), (0,)))
    grad_in = dot(d_proj, normed, ((1,), (1,)))
    grad_down = dot(act, back, ((1,), (1,)))
    grad_mlp = jnp.concatenate([grad_in, grad_down], 0)
    grad_mid = jnp.sum(d_normed * unit, axis=1, keepdims=True)
    d_unit = d_normed * gain_mid[:, None]
    d_level = back.astype(F32) + mid_scale * (d_unit - unit * jnp.mean(d_unit * unit, axis=0, keepdims=True))
    d_bf = d_level.astype(BF16)
    own_hot = (both[None, :] == bases).astype(BF16)
    d_low = (d_level - d_bf.astype(F32)).astype(BF16)
    base_sum = dot(d_bf, own_hot, ((1,), (1,))) + dot(d_low, own_hot, ((1,), (1,)))
    grad_filter = jnp.zeros(filt.shape, F32)
    kmer_sum = jnp.zeros((channels, half), F32)
    for s in range(2):
        d_scaled = dot(d_bf[:, s * local_len : (s + 1) * local_len], q_own, ((1,), (1,)))
        grad_filter = grad_filter + d_scaled * specs[s].astype(F32)
        d_spec = (filt * d_scaled).astype(BF16)
        kmer_sum = kmer_sum + dot(d_spec, hot_spec[s * half : (s + 1) * half], ((1,), (1,)))
    small = jnp.concatenate([base_sum, kmer_sum, grad_mid], 1)
    return layer_out, grad_mlp, grad_filter, small


def finish(small, embedding, gain_in, conv_taps):
    taps = conv_taps.shape[1]
    channels = embedding.shape[1]
    base_sum = small[:, :4].T
    kmer_sum = small[:, 4 : 4 + 4 * taps].reshape(channels, taps, 4)
    grad_mid = small[:, 4 + 4 * taps]
    base_scale = lax.rsqrt(jnp.mean(embedding * embedding, axis=1, keepdims=True) + 1e-6)
    unit = embedding * base_scale
    base_norm = (unit * gain_in[None, :]).astype(BF16).astype(F32)
    grad_conv = jnp.sum(kmer_sum * base_norm.T[:, None, :], axis=2)
    d_norm = jnp.sum(kmer_sum * conv_taps[:, :, None], axis=1).T
    grad_gain = jnp.sum(d_norm * unit, axis=0)
    d_unit = d_norm * gain_in[None, :]
    grad_emb = base_sum + base_scale * (d_unit - unit * jnp.mean(d_unit * unit, axis=1, keepdims=True))
    return grad_emb, grad_gain, grad_conv, grad_mid


def on_device(tokens, embedding, gain_in, conv_taps, long_filter, gain_mid, mlp_weights, cotangent):
    local_len = tokens.shape[1]
    block_len = long_filter.shape[1]
    rim = conv_taps.shape[1] - 1
    place = lax.axis_index("seq") * local_len
    block_start = place // block_len * block_len
    table = jnp.asarray(dct_table(block_len))
    q_own = lax.dynamic_slice(table, (0, place - block_start), (block_len, local_len))
    all_ids = lax.all_gather(tokens[0], "seq", axis=0, tiled=True)
    filt = lax.all_gather(long_filter.astype(BF16), "seq", axis=0, tiled=True).astype(F32)
    padded = jnp.pad(all_ids, (rim, rim), constant_values=4)
    ids_block = lax.dynamic_slice(padded, (block_start,), (block_len + 2 * rim,))
    layer_out, grad_mlp, grad_filter, small = compute(
        ids_block, tokens[0], table, q_own, embedding, gain_in, conv_taps, filt, gain_mid, mlp_weights, cotangent[0]
    )
    small = lax.psum(small, ("dp", "seq"))
    grad_emb, grad_gain, grad_conv, grad_mid = finish(small, embedding, gain_in, conv_taps)
    mine = lax.psum_scatter(grad_filter.astype(BF16), "seq", scatter_dimension=0, tiled=True)
    filter_out = lax.psum(mine, "dp").astype(F32)
    cols = lax.psum_scatter(grad_mlp.astype(BF16), "seq", scatter_dimension=1, tiled=True).astype(F32)
    mlp_out = lax.psum_scatter(cols, "dp", scatter_dimension=0, tiled=True)
    return layer_out[None], grad_emb, grad_gain, grad_conv, filter_out, grad_mid, mlp_out


def solution(mesh):
    placed = (P("dp", "seq"), P(), P(), P(), P("seq", None), P(), P(), P("dp", None, "seq"))
    return jax.shard_map(
        on_device,
        mesh=mesh,
        in_specs=placed,
        out_specs=(P("dp", None, "seq"), P(), P(), P(), P("seq", None), P(), P("dp", "seq")),
        check_vma=False,
    )
```

```python
import jax
import jax.numpy as jnp
import numpy as np
from jax import lax
from jax.experimental import pallas as pl
from jax.experimental.pallas import tpu as pltpu
from jax.sharding import PartitionSpec as P

F32 = jnp.float32
BF16 = jnp.bfloat16


def dct_table(length):
    freq = np.arange(length)[:, None]
    place = np.arange(length)[None, :]
    phase = (2 * place + 1) * freq % (4 * length)
    weight = np.where(freq == 0, np.sqrt(1.0 / length), np.sqrt(2.0 / length))
    return (weight * np.cos(np.pi * phase / (2 * length))).astype(np.float32).astype(BF16)


def dot(a, b, dims):
    return lax.dot_general(a, b, (dims, ((), ())), preferred_element_type=F32)


def compute(ids_block, ids_own, q_rows, q_own, embedding, gain_in, conv_taps, filt, gain_mid, mlp, cot):
    taps = conv_taps.shape[1]
    channels = embedding.shape[1]
    block_len = q_rows.shape[0]
    hidden = mlp.shape[0] // 3
    local_len = ids_own.shape[0]
    base_scale = lax.rsqrt(jnp.mean(embedding * embedding, axis=1, keepdims=True) + 1e-6)
    base_norm = (embedding * base_scale * gain_in[None, :]).astype(BF16)
    kmer = (conv_taps[:, :, None] * base_norm.astype(F32).T[:, None, :]).reshape(channels, -1).astype(BF16)
    bases = jnp.arange(4, dtype=jnp.int32)[:, None]
    rim = taps - 1
    fwd = [ids_block[rim - k : rim - k + block_len] for k in range(taps)]
    rev = [3 - ids_block[rim + k : rim + k + block_len] for k in range(taps)]
    hot = jnp.concatenate([(row[None, :] == bases) for row in fwd + rev], 0).astype(BF16)
    hot_spec = dot(hot, q_rows, ((1,), (1,))).astype(BF16)
    half = 4 * taps
    specs = [dot(kmer, hot_spec[s * half : (s + 1) * half], ((1,), (0,))).astype(BF16) for s in range(2)]
    scaled = [(filt * spec.astype(F32)).astype(BF16) for spec in specs]
    filtered = jnp.concatenate([dot(one, q_own, ((1,), (0,))) for one in scaled], 1)
    both = jnp.concatenate([ids_own, 3 - ids_own])
    emb_cols = embedding.T
    residual = jnp.zeros((channels, 2 * local_len), F32)
    for a in range(4):
        residual = residual + jnp.where(both[None, :] == a, emb_cols[:, a : a + 1], 0.0)
    level = residual + filtered
    mid_scale = lax.rsqrt(jnp.mean(level * level, axis=0, keepdims=True) + 1e-6)
    unit = level * mid_scale
    normed = (unit * gain_mid[:, None]).astype(BF16)
    w_in, w_down = mlp[: 2 * hidden], mlp[2 * hidden :]
    proj = dot(w_in, normed, ((1,), (0,))).astype(BF16).astype(F32)
    gate, up = proj[:hidden], proj[hidden:]
    sig = jax.nn.sigmoid(gate)
    act = (gate * sig * up).astype(BF16)
    combined = (level + dot(w_down, act, ((0,), (0,)))).astype(BF16)
    layer_out = jnp.concatenate([combined[:, :local_len], jnp.flip(combined[:, local_len:], 0)], 0)
    back = jnp.concatenate([cot[:channels], jnp.flip(cot[channels:], 0)], 1)
    d_act = dot(w_down, back, ((1,), (0,)))
    d_gate = d_act * up * sig * (1.0 + gate * (1.0 - sig))
    d_up = d_act * gate * sig
    d_proj = jnp.concatenate([d_gate, d_up], 0).astype(BF16)
    d_normed = dot(w_in, d_proj, ((0,), (0,)))
    grad_in = dot(d_proj, normed, ((1,), (1,)))
    grad_down = dot(act, back, ((1,), (1,)))
    grad_mlp = jnp.concatenate([grad_in, grad_down], 0)
    grad_mid = jnp.sum(d_normed * unit, axis=1, keepdims=True)
    d_unit = d_normed * gain_mid[:, None]
    d_level = back.astype(F32) + mid_scale * (d_unit - unit * jnp.mean(d_unit * unit, axis=0, keepdims=True))
    d_bf = d_level.astype(BF16)
    own_hot = (both[None, :] == bases).astype(BF16)
    d_low = (d_level - d_bf.astype(F32)).astype(BF16)
    base_sum = dot(d_bf, own_hot, ((1,), (1,))) + dot(d_low, own_hot, ((1,), (1,)))
    grad_filter = jnp.zeros(filt.shape, F32)
    kmer_sum = jnp.zeros((channels, half), F32)
    for s in range(2):
        d_scaled = dot(d_bf[:, s * local_len : (s + 1) * local_len], q_own, ((1,), (1,)))
        grad_filter = grad_filter + d_scaled * specs[s].astype(F32)
        d_spec = (filt * d_scaled).astype(BF16)
        kmer_sum = kmer_sum + dot(d_spec, hot_spec[s * half : (s + 1) * half], ((1,), (1,)))
    small = jnp.concatenate([base_sum, kmer_sum, grad_mid], 1).T
    return layer_out, grad_mlp, grad_filter, small


def finish(small, embedding, gain_in, conv_taps):
    taps = conv_taps.shape[1]
    channels = embedding.shape[1]
    base_sum = small[:, :4].T
    kmer_sum = small[:, 4 : 4 + 4 * taps].reshape(channels, taps, 4)
    grad_mid = small[:, 4 + 4 * taps]
    base_scale = lax.rsqrt(jnp.mean(embedding * embedding, axis=1, keepdims=True) + 1e-6)
    unit = embedding * base_scale
    base_norm = (unit * gain_in[None, :]).astype(BF16).astype(F32)
    grad_conv = jnp.sum(kmer_sum * base_norm.T[:, None, :], axis=2)
    d_norm = jnp.sum(kmer_sum * conv_taps[:, :, None], axis=1).T
    grad_gain = jnp.sum(d_norm * unit, axis=0)
    d_unit = d_norm * gain_in[None, :]
    grad_emb = base_sum + base_scale * (d_unit - unit * jnp.mean(d_unit * unit, axis=1, keepdims=True))
    return grad_emb, grad_gain, grad_conv, grad_mid


MESH = pl.DeviceIdType.MESH


def greet(dp_peers, seq_peers):
    barrier = pltpu.get_barrier_semaphore()
    for peer in dp_peers:
        pl.semaphore_signal(barrier, inc=1, device_id=peer, device_id_type=MESH)
    for peer in seq_peers:
        pl.semaphore_signal(barrier, inc=1, device_id=peer, device_id_type=MESH)
    pl.semaphore_wait(barrier, len(dp_peers) + len(seq_peers))


def remote(src, dst, send, recv, peer):
    return pltpu.make_async_remote_copy(
        src_ref=src, dst_ref=dst, send_sem=send, recv_sem=recv, device_id=peer, device_id_type=MESH
    )


def ring_of(at, count, spot):
    return [spot(lax.rem(at + off, count)) for off in range(1, count)]


def gather_kernel(n_seq, shard, ids, gath, all_ids, send, recv, swap_send, swap_recv, id_send, id_recv):
    dp, sq = lax.axis_index("dp"), lax.axis_index("seq")
    core = lax.rem(dp, 2)
    mate = (dp + 1 - 2 * core, sq)
    peers = ring_of(sq, n_seq, lambda j: (dp, j))
    greet([mate], peers)
    sends = []
    for off in range(1, n_seq):
        id_copy = remote(ids, all_ids.at[sq], id_send.at[off], id_recv.at[off], peers[off - 1])
        copy = remote(shard.at[core], gath.at[sq, core], send.at[off], recv.at[off], peers[off - 1])
        id_copy.start()
        copy.start()
        sends += [id_copy, copy]
    all_ids[sq] = ids[...]
    gath[sq] = shard[...]
    for off in [*range(n_seq - 1, 0, -1)]:
        source = lax.rem(sq - off + n_seq, n_seq)
        landed = gath.at[source, core]
        remote(landed, landed, send.at[off], recv.at[off], mate).wait_recv()
        swap = remote(landed, landed, swap_send.at[off], swap_recv.at[off], mate)
        swap.start()
        sends.append(swap)
    for off in range(1, n_seq):
        source = lax.rem(sq - off + n_seq, n_seq)
        other = gath.at[source, 1 - core]
        remote(other, other, swap_send.at[off], swap_recv.at[off], mate).wait_recv()
        got = all_ids.at[source]
        remote(got, got, id_send.at[off], id_recv.at[off], mate).wait_recv()
    for copy in sends:
        copy.wait_send()


def gather_all(n_seq, shard, ids):
    rows, width = shard.shape
    halves = shard.reshape(2, rows // 2, width)
    vmem = pl.BlockSpec(memory_space=pltpu.VMEM)
    dma = pltpu.SemaphoreType.DMA((n_seq,))
    gath, all_ids = pl.pallas_call(
        lambda *refs: gather_kernel(n_seq, *refs),
        out_shape=(
            jax.ShapeDtypeStruct((n_seq,) + halves.shape, shard.dtype),
            jax.ShapeDtypeStruct((n_seq,) + ids.shape, ids.dtype),
        ),
        in_specs=[vmem] * 2,
        out_specs=[vmem] * 2,
        scratch_shapes=[dma] * 6,
        compiler_params=pltpu.CompilerParams(collective_id=0, has_side_effects=True),
        name="gather",
    )(halves, ids)
    return gath.reshape(n_seq * rows, width), all_ids.reshape(-1)


def at_axis(axis, index):
    return (slice(None),) * axis + (index,)


def reduce_kernel(n_dp, n_seq, mlp_a, mlp_b, filt, small, mlp_out, filt_out, small_out, *scratch):
    bits = n_dp.bit_length() - 1
    stages = bits
    per = 2 * stages
    rec_a, rec_b, rec_f = scratch[0:stages], scratch[stages:per], scratch[per : per + stages]
    rest = scratch[per + stages :]
    acc_a, acc_b, acc_f = rest[0:stages], rest[stages:per], rest[per : per + stages]
    small_acc, small_rec, z_mlp, z_mlp_rec, z_f_rec, z_s_rec, mine, gath = rest[per + stages : per + stages + 8]
    send, recv, z_send, z_recv, g_send, g_recv = rest[per + stages + 8 :]
    dp, sq = lax.axis_index("dp"), lax.axis_index("seq")
    dp_peers = ring_of(dp, n_dp, lambda i: (i, sq))
    seq_peers = ring_of(sq, n_seq, lambda j: (dp, j))
    greet(dp_peers, seq_peers)
    order_a = [*range(bits)]
    order_b = [0] + [*range(2, bits)] + ([1] if bits > 1 else [])
    left_a = [*range(bits - 1, -1, -1)]
    left_b = [*range(bits - 1, -1, -1)]
    cur_a, cur_b, cur_f, cur_s = mlp_a, mlp_b, filt, small
    waits = []
    for stage in range(stages):
        bit_a, bit_b = order_a[stage], order_b[stage]
        my_a, my_b = lax.rem(dp // 2**bit_a, 2), lax.rem(dp // 2**bit_b, 2)
        to_a = (dp + (1 - 2 * my_a) * 2**bit_a, sq)
        to_b = (dp + (1 - 2 * my_b) * 2**bit_b, sq)
        ax_a, ax_b = left_a.index(bit_a), left_b.index(bit_b)
        copies = [
            remote(cur_a.at[at_axis(ax_a, 1 - my_a)], rec_a[stage], send.at[stage, 0], recv.at[stage, 0], to_a),
            remote(cur_f.at[at_axis(ax_b, 1 - my_b)], rec_f[stage], send.at[stage, 1], recv.at[stage, 1], to_b),
            remote(cur_b.at[at_axis(ax_b, 1 - my_b)], rec_b[stage], send.at[stage, 2], recv.at[stage, 2], to_b),
            remote(cur_s, small_rec.at[stage], send.at[stage, 3], recv.at[stage, 3], to_a),
        ]
        for copy in copies:
            copy.start()
        waits += copies
        copies[0].wait_recv()
        acc_a[stage][...] = (cur_a[at_axis(ax_a, my_a)].astype(F32) + rec_a[stage][...].astype(F32)).astype(BF16)
        copies[1].wait_recv()
        acc_f[stage][...] = (cur_f[at_axis(ax_b, my_b)].astype(F32) + rec_f[stage][...].astype(F32)).astype(BF16)
        copies[2].wait_recv()
        acc_b[stage][...] = (cur_b[at_axis(ax_b, my_b)].astype(F32) + rec_b[stage][...].astype(F32)).astype(BF16)
        copies[3].wait_recv()
        small_acc[stage] = cur_s[...] + small_rec[stage]
        cur_a, cur_b, cur_f, cur_s = acc_a[stage], acc_b[stage], acc_f[stage], small_acc.at[stage]
        left_a.remove(bit_a)
        left_b.remove(bit_b)
    joined = jnp.concatenate([cur_a[...], cur_b[...]], 1)
    cols = joined.shape[1] // n_seq
    for j in range(n_seq):
        z_mlp[j] = joined[:, j * cols : (j + 1) * cols]
    for off in range(1, n_seq):
        to = lax.rem(sq + off, n_seq)
        copies = [
            remote(cur_f.at[to], z_f_rec.at[off], z_send.at[0, off], z_recv.at[0, off], (dp, to)),
            remote(cur_s, z_s_rec.at[sq], z_send.at[1, off], z_recv.at[1, off], (dp, to)),
            remote(z_mlp.at[to], z_mlp_rec.at[off], z_send.at[2, off], z_recv.at[2, off], (dp, to)),
        ]
        for copy in copies:
            copy.start()
        waits += copies
    z_s_rec[sq] = cur_s[...]
    total = cur_f[sq].astype(F32)
    for off in range(1, n_seq):
        slot = z_f_rec.at[off]
        remote(slot, slot, z_send.at[0, off], z_recv.at[0, off], (dp, sq)).wait_recv()
        total = total + z_f_rec[off].astype(F32)
    mine[...] = total.astype(BF16)
    for off in range(1, n_dp):
        to = lax.rem(dp + off, n_dp)
        copy = remote(mine, gath.at[dp], g_send.at[off], g_recv.at[off], (to, sq))
        copy.start()
        waits.append(copy)
    gath[dp] = mine[...]
    for off in range(1, n_seq):
        source = lax.rem(sq - off + n_seq, n_seq)
        slot = z_s_rec.at[source]
        remote(slot, slot, z_send.at[1, off], z_recv.at[1, off], (dp, sq)).wait_recv()
        slot = z_mlp_rec.at[off]
        remote(slot, slot, z_send.at[2, off], z_recv.at[2, off], (dp, sq)).wait_recv()
    total = z_mlp[sq].astype(F32)
    for off in range(1, n_seq):
        total = total + z_mlp_rec[off].astype(F32)
    mlp_out[...] = total
    total = z_s_rec[0]
    for j in range(1, n_seq):
        total = total + z_s_rec[j]
    small_out[...] = total
    for off in range(1, n_dp):
        source = lax.rem(dp - off + n_dp, n_dp)
        slot = gath.at[source]
        remote(slot, slot, g_send.at[off], g_recv.at[off], (dp, sq)).wait_recv()
    filt_out[...] = gath[...].astype(F32)
    for copy in waits:
        copy.wait_send()


def reduce_all(n_dp, n_seq, grad_mlp, grad_filter, small):
    bits = n_dp.bit_length() - 1
    twos = (2,) * bits
    rows, width = grad_mlp.shape
    part = rows // n_dp
    lanes = 128
    cut = width // lanes * 2 // 3 * lanes
    mlp = grad_mlp.astype(BF16).reshape(twos + (part, width))
    mlp_a, mlp_b = mlp[..., :cut], mlp[..., cut:]
    chan, length = grad_filter.shape
    own = chan // n_seq
    tidy = length % (n_dp * lanes) == 0
    filt = grad_filter.astype(BF16)
    if tidy:
        filt = filt.reshape(n_seq, own, n_dp, length // n_dp).transpose(2, 0, 1, 3)
    else:
        filt = filt.reshape(n_seq, n_dp, -1, lanes).transpose(1, 0, 2, 3)
    f_tail = filt.shape[1:]
    filt = filt.reshape(twos + f_tail)

    def halves(tail):
        return [pltpu.VMEM(twos[stage + 1 :] + tail, BF16) for stage in range(bits)]

    tails = [(part, cut), (part, width - cut), f_tail]
    buffers = [b for tail in tails for b in halves(tail)]
    cols = width // n_seq
    dma = pltpu.SemaphoreType.DMA
    vmem = pl.BlockSpec(memory_space=pltpu.VMEM)
    mlp_out, filt_out, small_out = pl.pallas_call(
        lambda *refs: reduce_kernel(n_dp, n_seq, *refs),
        out_shape=(
            jax.ShapeDtypeStruct((part, cols), F32),
            jax.ShapeDtypeStruct((n_dp,) + f_tail[1:], F32),
            jax.ShapeDtypeStruct(small.shape, F32),
        ),
        in_specs=[vmem] * 4,
        out_specs=[vmem] * 3,
        scratch_shapes=buffers * 2
        + [
            pltpu.VMEM((bits,) + small.shape, F32),
            pltpu.VMEM((bits,) + small.shape, F32),
            pltpu.VMEM((n_seq, part, cols), BF16),
            pltpu.VMEM((n_seq, part, cols), BF16),
            pltpu.VMEM(f_tail, BF16),
            pltpu.VMEM((n_seq,) + small.shape, F32),
            pltpu.VMEM(f_tail[1:], BF16),
            pltpu.VMEM((n_dp,) + f_tail[1:], BF16),
            dma((bits, 4)),
            dma((bits, 4)),
            dma((3, n_seq)),
            dma((3, n_seq)),
            dma((n_dp,)),
            dma((n_dp,)),
        ],
        compiler_params=pltpu.CompilerParams(collective_id=1, has_side_effects=True, vmem_limit_bytes=50 * 2**20),
        name="reduce",
    )(mlp_a, mlp_b, filt, small)
    if tidy:
        filt_out = filt_out.transpose(1, 0, 2)
    return mlp_out, filt_out.reshape(own, length), small_out


def on_device(tokens, embedding, gain_in, conv_taps, long_filter, gain_mid, mlp_weights, cotangent):
    local_len = tokens.shape[1]
    block_len = long_filter.shape[1]
    rim = conv_taps.shape[1] - 1
    place = lax.axis_index("seq") * local_len
    block_start = place // block_len * block_len
    table = jnp.asarray(dct_table(block_len))
    q_own = lax.dynamic_slice(table, (0, place - block_start), (block_len, local_len))
    n_dp, n_seq = lax.axis_size("dp"), lax.axis_size("seq")
    filt, all_ids = gather_all(n_seq, long_filter.astype(BF16), tokens)
    filt = filt.astype(F32)
    padded = jnp.pad(all_ids, (rim, rim), constant_values=4)
    ids_block = lax.dynamic_slice(padded, (block_start,), (block_len + 2 * rim,))
    layer_out, grad_mlp, grad_filter, small = compute(
        ids_block, tokens[0], table, q_own, embedding, gain_in, conv_taps, filt, gain_mid, mlp_weights, cotangent[0]
    )
    mlp_out, filter_out, small = reduce_all(n_dp, n_seq, grad_mlp, grad_filter, small)
    grad_emb, grad_gain, grad_conv, grad_mid = finish(small.T, embedding, gain_in, conv_taps)
    return layer_out[None], grad_emb, grad_gain, grad_conv, filter_out, grad_mid, mlp_out


def solution(mesh):
    placed = (P("dp", "seq"), P(), P(), P(), P("seq", None), P(), P(), P("dp", None, "seq"))
    return jax.shard_map(
        on_device,
        mesh=mesh,
        in_specs=placed,
        out_specs=(P("dp", None, "seq"), P(), P(), P(), P("seq", None), P(), P("dp", "seq")),
        check_vma=False,
    )
```

```python
import jax
import jax.numpy as jnp
import numpy as np
from jax import lax
from jax.experimental import pallas as pl
from jax.experimental.pallas import tpu as pltpu
from jax.sharding import PartitionSpec as P

F32 = jnp.float32
BF16 = jnp.bfloat16


def dct_table(length):
    freq = np.arange(length)[:, None]
    place = np.arange(length)[None, :]
    phase = (2 * place + 1) * freq % (4 * length)
    weight = np.where(freq == 0, np.sqrt(1.0 / length), np.sqrt(2.0 / length))
    return (weight * np.cos(np.pi * phase / (2 * length))).astype(np.float32).astype(BF16)


def dot(a, b, dims):
    return lax.dot_general(a, b, (dims, ((), ())), preferred_element_type=F32)


def local_kernel(
    n_seq, n_dp, tidy, all_ids, ids, table, emb_cols, gain_in, taps, filt, gain_mid, mlp, cot,
    out, mlp_a, mlp_b, filt_out, small, full, spec_ref, level_ref, normed_ref, d_normed_ref, down_ref,
):
    channels, block_len = filt.shape[0] * filt.shape[1], filt.shape[2]
    local_len = ids.shape[1]
    hidden = mlp.shape[0] // 3
    n_taps = taps.shape[1]
    half = 4 * n_taps
    cut = mlp_a.shape[1]
    place = lax.axis_index("seq")
    per_block = block_len // local_len
    first = place // per_block * per_block
    last = first + per_block - 1
    offset = pl.multiple_of((place - first) * local_len, local_len)
    emb = emb_cols[...]
    base_scale = lax.rsqrt(jnp.mean(emb * emb, axis=0, keepdims=True) + 1e-6)
    base_norm = (emb * base_scale * gain_in[...]).astype(BF16).astype(F32)
    lane = lax.broadcasted_iota(jnp.int32, (channels, half), 1)
    tap_part = jnp.zeros((channels, half), F32)
    base_part = jnp.zeros((channels, half), F32)
    for k in range(n_taps):
        tap_part = jnp.where(lane // 4 == k, taps[:, k : k + 1], tap_part)
    for a in range(4):
        base_part = jnp.where(lane % 4 == a, base_norm[:, a : a + 1], base_part)
    kmer = (tap_part * base_part).astype(BF16)
    edge = 128
    before = jnp.where(first > 0, all_ids[jnp.maximum(first - 1, 0)][:, local_len - edge :], 4)
    after = jnp.where(last < n_seq - 1, all_ids[jnp.minimum(last + 1, n_seq - 1)][:, :edge], 4)
    row = jnp.concatenate([before] + [all_ids[first + j] for j in range(per_block)] + [after], 1)
    width = block_len + 2 * edge
    wide = jnp.broadcast_to(row, (8, width))
    sub = lax.broadcasted_iota(jnp.int32, (8, block_len), 0)
    tiles = []
    for s in range(2):
        for k in range(0, n_taps, 2):
            shifts = [(k + i) if s == 0 else (width - k - i) % width for i in range(2)]
            moved = [(pltpu.roll(wide, sh, 1) if sh else wide)[:, edge : edge + block_len] for sh in shifts]
            picked = jnp.where(sub < 4, moved[0], moved[1])
            want = sub % 4 if s == 0 else 3 - sub % 4
            tiles.append(jnp.where(picked == want, 1.0, 0.0))
    hot = jnp.concatenate(tiles, 0).astype(BF16)
    hot_spec = dot(hot, table[...], ((1,), (0,))).astype(BF16)
    rows = filt.shape[1]
    for j in range(n_seq):
        full[j * rows : (j + 1) * rows, :] = filt[j].astype(F32)
    own = ids[...]
    emb_all = emb_cols[...]
    q_own = table[pl.ds(offset, local_len), :]
    for s in range(2):
        spec = dot(kmer, hot_spec[s * half : (s + 1) * half], ((1,), (0,))).astype(BF16)
        spec_ref[s] = spec
        scaled = (full[...] * spec.astype(F32)).astype(BF16)
        mine = own if s == 0 else 3 - own
        level = dot(scaled, q_own, ((1,), (1,)))
        residual = jnp.zeros((channels, local_len), F32)
        for a in range(4):
            residual = jnp.where(mine == a, emb_all[:, a : a + 1], residual)
        level_ref[:, s * local_len : (s + 1) * local_len] = level + residual
    level = level_ref[...]
    mid_scale = lax.rsqrt(jnp.mean(level * level, axis=0, keepdims=True) + 1e-6)
    normed_ref[...] = (level * mid_scale * gain_mid[...]).astype(BF16)
    turn = jnp.where(
        lax.broadcasted_iota(jnp.int32, (channels, channels), 0)
        + lax.broadcasted_iota(jnp.int32, (channels, channels), 1)
        == channels - 1,
        1.0,
        0.0,
    ).astype(BF16)
    turned = dot(turn, cot[channels:, :], ((1,), (0,))).astype(BF16)
    back = jnp.concatenate([cot[:channels, :], turned], 1)
    normed = normed_ref[...]
    tile = 256 if hidden % 256 == 0 else hidden
    for t in range(hidden // tile):
        g0, u0, w0 = t * tile, hidden + t * tile, 2 * hidden + t * tile
        w_gate, w_up, w_down = mlp[g0 : g0 + tile, :], mlp[u0 : u0 + tile, :], mlp[w0 : w0 + tile, :]
        gate = dot(w_gate, normed, ((1,), (0,)))
        up = dot(w_up, normed, ((1,), (0,)))
        d_act = dot(w_down, back, ((1,), (0,)))
        sig = jax.nn.sigmoid(gate)
        silu = gate * sig
        act = (silu * up).astype(BF16)
        d_gate = (d_act * up * (sig + silu * (1.0 - sig))).astype(BF16)
        d_up = (d_act * silu).astype(BF16)
        down = dot(w_down, act, ((0,), (0,)))
        down_ref[...] = down if t == 0 else down_ref[...] + down
        d_part = dot(w_gate, d_gate, ((0,), (0,))) + dot(w_up, d_up, ((0,), (0,)))
        d_normed_ref[...] = d_part if t == 0 else d_normed_ref[...] + d_part
        for start, left, right in ((g0, d_gate, normed), (u0, d_up, normed), (w0, act, back)):
            grad = dot(left, right, ((1,), (1,))).astype(BF16)
            mlp_a[start : start + tile, :] = grad[:, :cut]
            mlp_b[start : start + tile, :] = grad[:, cut:]
    combined = (level_ref[...] + down_ref[...]).astype(BF16)
    out[:channels, :] = combined[:, :local_len]
    out[channels:, :] = dot(turn, combined[:, local_len:], ((1,), (0,))).astype(BF16)
    unit = level * mid_scale
    d_normed = d_normed_ref[...]
    mid_grad = d_normed * unit
    d_unit = d_normed * gain_mid[...]
    d_level = back.astype(F32) + mid_scale * (d_unit - unit * jnp.mean(d_unit * unit, axis=0, keepdims=True))
    d_bf = d_level.astype(BF16)
    d_low = (d_level - d_bf.astype(F32)).astype(BF16)
    both = jnp.concatenate([own, 3 - own], 1)
    sub8 = lax.broadcasted_iota(jnp.int32, (8, 2 * local_len), 0)
    own_hot = jnp.where(sub8 == both, 1.0, 0.0).astype(BF16)
    ones = jnp.ones((8, 2 * local_len), BF16)
    m_bf = mid_grad.astype(BF16)
    m_low = (mid_grad - m_bf.astype(F32)).astype(BF16)
    small[half : half + 8, :] = dot(own_hot, d_bf, ((1,), (1,))) + dot(own_hot, d_low, ((1,), (1,)))
    small[half + 8 : half + 16, :] = dot(ones, m_bf, ((1,), (1,))) + dot(ones, m_low, ((1,), (1,)))
    q_rows = table[pl.ds(offset, local_len), :]
    grad_filter = jnp.zeros((channels, block_len), F32)
    kmer_sum = jnp.zeros((half, channels), F32)
    for s in range(2):
        d_scaled = dot(d_bf[:, s * local_len : (s + 1) * local_len], q_rows, ((1,), (0,)))
        grad_filter = grad_filter + d_scaled * spec_ref[s].astype(F32)
        d_spec = (full[...] * d_scaled).astype(BF16)
        kmer_sum = kmer_sum + dot(hot_spec[s * half : (s + 1) * half], d_spec, ((1,), (1,)))
    small[:half, :] = kmer_sum
    grad_filter = grad_filter.astype(BF16)
    if tidy:
        piece = block_len // n_dp
        for i in range(n_dp):
            filt_out[i] = grad_filter[:, i * piece : (i + 1) * piece]
    else:
        filt_out[...] = grad_filter


def compute(n_seq, n_dp, all_ids, ids, embedding, gain_in, conv_taps, filt, gain_mid, mlp, cot):
    channels = embedding.shape[1]
    block_len = filt.shape[-1]
    local_len = ids.shape[1]
    table = jnp.asarray(dct_table(block_len).T)
    cut = channels // 128 * 2 // 3 * 128
    tidy = block_len % (n_dp * 128) == 0
    f_shape = (n_dp, channels, block_len // n_dp) if tidy else (channels, block_len)
    sums = 4 * conv_taps.shape[1] + 16
    vmem = pl.BlockSpec(memory_space=pltpu.VMEM)
    return pl.pallas_call(
        lambda *refs: local_kernel(n_seq, n_dp, tidy, *refs),
        out_shape=(
            jax.ShapeDtypeStruct(cot.shape, BF16),
            jax.ShapeDtypeStruct((mlp.shape[0], cut), BF16),
            jax.ShapeDtypeStruct((mlp.shape[0], channels - cut), BF16),
            jax.ShapeDtypeStruct(f_shape, BF16),
            jax.ShapeDtypeStruct((sums, channels), F32),
        ),
        in_specs=[vmem] * 10,
        out_specs=[vmem] * 5,
        scratch_shapes=[
            pltpu.VMEM((channels, block_len), F32),
            pltpu.VMEM((2, channels, block_len), BF16),
            pltpu.VMEM((channels, 2 * local_len), F32),
            pltpu.VMEM((channels, 2 * local_len), BF16),
            pltpu.VMEM((channels, 2 * local_len), F32),
            pltpu.VMEM((channels, 2 * local_len), F32),
        ],
        compiler_params=pltpu.CompilerParams(vmem_limit_bytes=58 * 2**20),
        name="local",
    )(all_ids, ids, table, embedding.T, gain_in[:, None], conv_taps, filt, gain_mid[:, None], mlp, cot)


def finish_kernel(small, embedding, gain_in, taps, grad_emb, grad_gain, grad_conv, grad_mid):
    n_taps = taps.shape[0]
    emb = embedding[...]
    base_scale = lax.rsqrt(jnp.mean(emb * emb, axis=1, keepdims=True) + 1e-6)
    unit = emb * base_scale
    base_norm = (unit * gain_in[...]).astype(BF16).astype(F32)
    d_norm = jnp.zeros(emb.shape, F32)
    for k in range(n_taps):
        part = small[4 * k : 4 * k + 4, :]
        d_norm = d_norm + part * taps[k : k + 1, :]
        grad_conv[k : k + 1, :] = jnp.sum(part * base_norm, axis=0, keepdims=True)
    grad_gain[...] = jnp.sum(d_norm * unit, axis=0, keepdims=True)
    d_unit = d_norm * gain_in[...]
    base_sum = small[4 * n_taps : 4 * n_taps + 4, :]
    grad_emb[...] = base_sum + base_scale * (d_unit - unit * jnp.mean(d_unit * unit, axis=1, keepdims=True))
    grad_mid[...] = small[4 * n_taps + 8 : 4 * n_taps + 9, :]


def finish(small, embedding, gain_in, conv_taps):
    row = jax.ShapeDtypeStruct((1, embedding.shape[1]), F32)
    vmem = pl.BlockSpec(memory_space=pltpu.VMEM)
    grad_emb, grad_gain, grad_conv, grad_mid = pl.pallas_call(
        finish_kernel,
        out_shape=(jax.ShapeDtypeStruct(embedding.shape, F32), row, jax.ShapeDtypeStruct(conv_taps.shape[::-1], F32), row),
        in_specs=[vmem] * 4,
        out_specs=[vmem] * 4,
        name="finish",
    )(small, embedding, gain_in[None, :], conv_taps.T)
    return grad_emb, grad_gain[0], grad_conv.T, grad_mid[0]


MESH = pl.DeviceIdType.MESH


def greet(dp_peers, seq_peers):
    barrier = pltpu.get_barrier_semaphore()
    for peer in dp_peers:
        pl.semaphore_signal(barrier, inc=1, device_id=peer, device_id_type=MESH)
    for peer in seq_peers:
        pl.semaphore_signal(barrier, inc=1, device_id=peer, device_id_type=MESH)
    pl.semaphore_wait(barrier, len(dp_peers) + len(seq_peers))


def remote(src, dst, send, recv, peer):
    return pltpu.make_async_remote_copy(
        src_ref=src, dst_ref=dst, send_sem=send, recv_sem=recv, device_id=peer, device_id_type=MESH
    )


def ring_of(at, count, spot):
    return [spot(lax.rem(at + off, count)) for off in range(1, count)]


def gather_kernel(n_seq, shard, ids, gath, all_ids, send, recv, swap_send, swap_recv, id_send, id_recv):
    dp, sq = lax.axis_index("dp"), lax.axis_index("seq")
    core = lax.rem(dp, 2)
    mate = (dp + 1 - 2 * core, sq)
    peers = ring_of(sq, n_seq, lambda j: (dp, j))
    gath[sq] = shard[...].astype(BF16)
    wide = shard.shape[1] // 2
    low = pl.multiple_of(core * wide, wide)
    high = pl.multiple_of((1 - core) * wide, wide)
    greet([mate], peers)
    sends = []
    for off in range(1, n_seq):
        id_copy = remote(ids, all_ids.at[sq], id_send.at[off], id_recv.at[off], peers[off - 1])
        part = gath.at[sq, :, pl.ds(low, wide)]
        copy = remote(part, part, send.at[off], recv.at[off], peers[off - 1])
        id_copy.start()
        copy.start()
        sends += [id_copy, copy]
    all_ids[sq] = ids[...]
    for off in [*range(n_seq - 1, 0, -1)]:
        source = lax.rem(sq - off + n_seq, n_seq)
        landed = gath.at[source, :, pl.ds(low, wide)]
        remote(landed, landed, send.at[off], recv.at[off], mate).wait_recv()
        swap = remote(landed, landed, swap_send.at[off], swap_recv.at[off], mate)
        swap.start()
        sends.append(swap)
    for off in range(1, n_seq):
        source = lax.rem(sq - off + n_seq, n_seq)
        other = gath.at[source, :, pl.ds(high, wide)]
        remote(other, other, swap_send.at[off], swap_recv.at[off], mate).wait_recv()
        got = all_ids.at[source]
        remote(got, got, id_send.at[off], id_recv.at[off], mate).wait_recv()
    for copy in sends:
        copy.wait_send()


def gather_all(n_seq, shard, ids):
    rows, width = shard.shape
    vmem = pl.BlockSpec(memory_space=pltpu.VMEM)
    dma = pltpu.SemaphoreType.DMA((n_seq,))
    gath, all_ids = pl.pallas_call(
        lambda *refs: gather_kernel(n_seq, *refs),
        out_shape=(
            jax.ShapeDtypeStruct((n_seq, rows, width), BF16),
            jax.ShapeDtypeStruct((n_seq,) + ids.shape, ids.dtype),
        ),
        in_specs=[vmem] * 2,
        out_specs=[vmem] * 2,
        scratch_shapes=[dma] * 6,
        compiler_params=pltpu.CompilerParams(collective_id=0, has_side_effects=True),
        name="gather",
    )(shard, ids)
    return gath, all_ids


def at_axis(axis, index):
    return (slice(None),) * axis + (index,)


def reduce_kernel(n_dp, n_seq, mlp_a, mlp_b, filt, small, mlp_out, filt_out, small_out, *scratch):
    bits = n_dp.bit_length() - 1
    stages = bits
    per = 2 * stages
    rec_a, rec_b, rec_f = scratch[0:stages], scratch[stages:per], scratch[per : per + stages]
    rest = scratch[per + stages :]
    acc_a, acc_b, acc_f = rest[0:stages], rest[stages:per], rest[per : per + stages]
    small_acc, small_rec, z_mlp, z_mlp_rec, z_f_rec, z_s_rec, mine, gath = rest[per + stages : per + stages + 8]
    send, recv, z_send, z_recv, g_send, g_recv = rest[per + stages + 8 :]
    dp, sq = lax.axis_index("dp"), lax.axis_index("seq")
    dp_peers = ring_of(dp, n_dp, lambda i: (i, sq))
    seq_peers = ring_of(sq, n_seq, lambda j: (dp, j))
    greet(dp_peers, seq_peers)
    order_a = [*range(bits)]
    order_b = [0] + [*range(2, bits)] + ([1] if bits > 1 else [])
    left_a = [*range(bits - 1, -1, -1)]
    left_b = [*range(bits - 1, -1, -1)]
    cur_a, cur_b, cur_f, cur_s = mlp_a, mlp_b, filt, small
    waits = []
    for stage in range(stages):
        bit_a, bit_b = order_a[stage], order_b[stage]
        my_a, my_b = lax.rem(dp // 2**bit_a, 2), lax.rem(dp // 2**bit_b, 2)
        to_a = (dp + (1 - 2 * my_a) * 2**bit_a, sq)
        to_b = (dp + (1 - 2 * my_b) * 2**bit_b, sq)
        ax_a, ax_b = left_a.index(bit_a), left_b.index(bit_b)
        copies = [
            remote(cur_a.at[at_axis(ax_a, 1 - my_a)], rec_a[stage], send.at[stage, 0], recv.at[stage, 0], to_a),
            remote(cur_f.at[at_axis(ax_b, 1 - my_b)], rec_f[stage], send.at[stage, 1], recv.at[stage, 1], to_b),
            remote(cur_b.at[at_axis(ax_b, 1 - my_b)], rec_b[stage], send.at[stage, 2], recv.at[stage, 2], to_b),
            remote(cur_s, small_rec.at[stage], send.at[stage, 3], recv.at[stage, 3], to_a),
        ]
        for copy in copies:
            copy.start()
        waits += copies
        copies[0].wait_recv()
        acc_a[stage][...] = (cur_a[at_axis(ax_a, my_a)].astype(F32) + rec_a[stage][...].astype(F32)).astype(BF16)
        copies[1].wait_recv()
        acc_f[stage][...] = (cur_f[at_axis(ax_b, my_b)].astype(F32) + rec_f[stage][...].astype(F32)).astype(BF16)
        copies[2].wait_recv()
        acc_b[stage][...] = (cur_b[at_axis(ax_b, my_b)].astype(F32) + rec_b[stage][...].astype(F32)).astype(BF16)
        copies[3].wait_recv()
        small_acc[stage] = cur_s[...] + small_rec[stage]
        cur_a, cur_b, cur_f, cur_s = acc_a[stage], acc_b[stage], acc_f[stage], small_acc.at[stage]
        left_a.remove(bit_a)
        left_b.remove(bit_b)
    joined = jnp.concatenate([cur_a[...], cur_b[...]], 1)
    cols = joined.shape[1] // n_seq
    for j in range(n_seq):
        z_mlp[j] = joined[:, j * cols : (j + 1) * cols]
    for off in range(1, n_seq):
        to = lax.rem(sq + off, n_seq)
        copies = [
            remote(cur_f.at[to], z_f_rec.at[off], z_send.at[0, off], z_recv.at[0, off], (dp, to)),
            remote(cur_s, z_s_rec.at[sq], z_send.at[1, off], z_recv.at[1, off], (dp, to)),
            remote(z_mlp.at[to], z_mlp_rec.at[off], z_send.at[2, off], z_recv.at[2, off], (dp, to)),
        ]
        for copy in copies:
            copy.start()
        waits += copies
    z_s_rec[sq] = cur_s[...]
    total = cur_f[sq].astype(F32)
    for off in range(1, n_seq):
        slot = z_f_rec.at[off]
        remote(slot, slot, z_send.at[0, off], z_recv.at[0, off], (dp, sq)).wait_recv()
        total = total + z_f_rec[off].astype(F32)
    mine[...] = total.astype(BF16)
    for off in range(1, n_dp):
        to = lax.rem(dp + off, n_dp)
        copy = remote(mine, gath.at[dp], g_send.at[off], g_recv.at[off], (to, sq))
        copy.start()
        waits.append(copy)
    gath[dp] = mine[...]
    for off in range(1, n_seq):
        source = lax.rem(sq - off + n_seq, n_seq)
        slot = z_s_rec.at[source]
        remote(slot, slot, z_send.at[1, off], z_recv.at[1, off], (dp, sq)).wait_recv()
        slot = z_mlp_rec.at[off]
        remote(slot, slot, z_send.at[2, off], z_recv.at[2, off], (dp, sq)).wait_recv()
    total = z_mlp[sq].astype(F32)
    for off in range(1, n_seq):
        total = total + z_mlp_rec[off].astype(F32)
    mlp_out[...] = total
    total = z_s_rec[0]
    for j in range(1, n_seq):
        total = total + z_s_rec[j]
    small_out[...] = total
    for off in range(1, n_dp):
        source = lax.rem(dp - off + n_dp, n_dp)
        slot = gath.at[source]
        remote(slot, slot, g_send.at[off], g_recv.at[off], (dp, sq)).wait_recv()
    filt_out[...] = gath[...].astype(F32)
    for copy in waits:
        copy.wait_send()


def reduce_all(n_dp, n_seq, mlp_a, mlp_b, filt, small):
    bits = n_dp.bit_length() - 1
    twos = (2,) * bits
    lanes = 128
    rows, cut = mlp_a.shape
    width = cut + mlp_b.shape[1]
    part = rows // n_dp
    mlp_a = mlp_a.reshape(twos + (part, cut))
    mlp_b = mlp_b.reshape(twos + (part, width - cut))
    tidy = filt.ndim == 3
    chan = filt.shape[-2]
    length = filt.shape[-1] * (n_dp if tidy else 1)
    own = chan // n_seq
    if tidy:
        filt = filt.reshape(n_dp, n_seq, own, length // n_dp)
    else:
        filt = filt.reshape(n_seq, n_dp, -1, lanes).transpose(1, 0, 2, 3)
    f_tail = filt.shape[1:]
    filt = filt.reshape(twos + f_tail)

    def halves(tail):
        return [pltpu.VMEM(twos[stage + 1 :] + tail, BF16) for stage in range(bits)]

    tails = [(part, cut), (part, width - cut), f_tail]
    buffers = [b for tail in tails for b in halves(tail)]
    cols = width // n_seq
    dma = pltpu.SemaphoreType.DMA
    vmem = pl.BlockSpec(memory_space=pltpu.VMEM)
    mlp_out, filt_out, small_out = pl.pallas_call(
        lambda *refs: reduce_kernel(n_dp, n_seq, *refs),
        out_shape=(
            jax.ShapeDtypeStruct((part, cols), F32),
            jax.ShapeDtypeStruct((n_dp,) + f_tail[1:], F32),
            jax.ShapeDtypeStruct(small.shape, F32),
        ),
        in_specs=[vmem] * 4,
        out_specs=[vmem] * 3,
        scratch_shapes=buffers * 2
        + [
            pltpu.VMEM((bits,) + small.shape, F32),
            pltpu.VMEM((bits,) + small.shape, F32),
            pltpu.VMEM((n_seq, part, cols), BF16),
            pltpu.VMEM((n_seq, part, cols), BF16),
            pltpu.VMEM(f_tail, BF16),
            pltpu.VMEM((n_seq,) + small.shape, F32),
            pltpu.VMEM(f_tail[1:], BF16),
            pltpu.VMEM((n_dp,) + f_tail[1:], BF16),
            dma((bits, 4)),
            dma((bits, 4)),
            dma((3, n_seq)),
            dma((3, n_seq)),
            dma((n_dp,)),
            dma((n_dp,)),
        ],
        compiler_params=pltpu.CompilerParams(collective_id=1, has_side_effects=True, vmem_limit_bytes=50 * 2**20),
        name="reduce",
    )(mlp_a, mlp_b, filt, small)
    if tidy:
        filt_out = filt_out.transpose(1, 0, 2)
    return mlp_out, filt_out.reshape(own, length), small_out


def on_device(tokens, embedding, gain_in, conv_taps, long_filter, gain_mid, mlp_weights, cotangent):
    n_dp, n_seq = lax.axis_size("dp"), lax.axis_size("seq")
    filt, all_ids = gather_all(n_seq, long_filter, tokens)
    layer_out, mlp_a, mlp_b, grad_filter, small = compute(
        n_seq, n_dp, all_ids, tokens, embedding, gain_in, conv_taps, filt, gain_mid, mlp_weights, cotangent[0]
    )
    mlp_out, filter_out, small = reduce_all(n_dp, n_seq, mlp_a, mlp_b, grad_filter, small)
    grad_emb, grad_gain, grad_conv, grad_mid = finish(small, embedding, gain_in, conv_taps)
    return layer_out[None], grad_emb, grad_gain, grad_conv, filter_out, grad_mid, mlp_out


def solution(mesh):
    placed = (P("dp", "seq"), P(), P(), P(), P("seq", None), P(), P(), P("dp", None, "seq"))
    return jax.shard_map(
        on_device,
        mesh=mesh,
        in_specs=placed,
        out_specs=(P("dp", None, "seq"), P(), P(), P(), P("seq", None), P(), P("dp", "seq")),
        check_vma=False,
    )
```
